512 devices in a mesh: vocab: 16 (over y, core), rows: 8 (over z), seq: 4 (over x).
Axes of the slice: x: 4, y: 8, z: 8, core: 2. Of those that a mesh axis runs over, the one named last changes fastest.
Arguments:
- hidden: bfloat16 [1024, 16384], P(('vocab', 'seq'), 'rows'), may hold values from -7 to 7
- head_weight: bfloat16 [16384, 65536], P('rows', ('vocab', 'seq')), may hold values from -0.1 to 0.1
- tokens: int32 [1024], P(('rows', 'seq')), may hold values from 0 to 65535
Outputs:
- logprobs: float32 [1024, 65536], P(('rows', 'seq'), 'vocab')
- target_logp: float32 [1024], P(('rows', 'seq'))
The draws below stay inside these ranges and needn't reach their ends.
All inputs are finite; a program needn't handle non-finite values.
Results may differ from the reference program's by a relative error of at most 0.0003.
Values may be sent and summed in bfloat16 or wider, within the bound.
No kernel may reach another device: no remote copies, remote signals or barrier semaphores. Data moves between devices by JAX's collectives and lax.ppermute only.
A program may use at most 64 MiB of HBM per device.

```python
import math
import jax
import jax.numpy as jnp
import numpy as np

D = 16384
R = 1024
V = 65536


def hidden_values(key):
    base_key = jax.random.fold_in(key, 11)
    return jnp.clip(jax.random.normal(base_key, (R, D), jnp.float32), -6.0, 6.0)


def draw_hidden(key, part):
    return hidden_values(key).astype(jnp.bfloat16)


def draw_head_weight(key, part):
    weights = jnp.clip(jax.random.normal(jax.random.fold_in(key, 23), (D, V), jnp.float32), -4.0, 4.0) * (3.0 / math.sqrt(D))
    return weights.astype(jnp.bfloat16)


def with_ends(drawn, stream_key, low, top_value):
    index_at = [jax.random.randint(jax.random.fold_in(stream_key, axis), (), 0, length) for axis, length in enumerate(drawn.shape)]
    widest = drawn.shape.index(max(drawn.shape))
    beside = index_at[:widest] + [(index_at[widest] + 1) % drawn.shape[widest]] + index_at[widest + 1:]
    return drawn.at[tuple(index_at)].set(low).at[tuple(beside)].set(top_value)


def cumulative_ranks(number_of, slope):
    weights = [(1 << 20) // math.isqrt(grade ** slope) + 1 for grade in range(1, number_of + 1)]
    width = 1 + sum(weights) // (1 << 30)
    return np.cumsum(np.array([max(1, weight // width) for weight in weights]))


def ranked(rng, dims, number_of, lean):
    listing = cumulative_ranks(number_of, lean)
    lot = jax.random.randint(jax.random.fold_in(rng, 1), dims, 0, int(listing[number_of - 1]))
    grade = jnp.searchsorted(jnp.asarray(listing, jnp.int32), lot, side="right")
    return jax.random.permutation(jax.random.fold_in(rng, 2), number_of)[grade].astype(jnp.int32)


def setup_inputs(seed: int = 0) -> dict:
    streams_of = jax.random.split(jax.random.key(seed), 4)
    return {
        "hidden": draw_hidden(jax.random.fold_in(streams_of[3], 71), 0),
        "head_weight": draw_head_weight(jax.random.fold_in(streams_of[3], 71), 0),
        "tokens": with_ends(ranked(streams_of[2], (R,), V, 2), jax.random.fold_in(streams_of[2], 3), 0, V - 1).astype(jnp.int32),
    }


def reference(hidden, head_weight, tokens):
    logits = jnp.dot(hidden, head_weight, preferred_element_type=jnp.float32)
    row_peak = jnp.max(logits, axis=1, keepdims=True)
    row_total = jnp.sum(jnp.exp(logits - row_peak), axis=1, keepdims=True)
    logprobs = logits - row_peak - jnp.log(row_total)
    target_logp = jnp.take_along_axis(logprobs, tokens[:, None].astype(jnp.int32), axis=1)[:, 0]
    return logprobs, target_logp
```

```python
import jax
import jax.numpy as jnp
from jax import lax
from jax.sharding import Mesh, PartitionSpec as P

F16 = jnp.float16
F32 = jnp.float32


def spread(x, axis, size):
    return lax.all_to_all(jnp.broadcast_to(x[None], (size,) + x.shape), axis, split_axis=0, concat_axis=0, tiled=True)


def local(ny, nz, nx, hidden, head_weight, tokens):
    n, k = hidden.shape
    cols = head_weight.shape[1]
    core = lax.axis_index("core")
    mine = spread(spread(hidden, "y", ny), "x", nx)
    mine = jnp.swapaxes(mine, 0, 1).reshape(ny * nx * n, k)
    other = lax.ppermute(mine, "core", [(0, 1), (1, 0)])

    def reduced(rows):
        part = jnp.dot(rows, head_weight, preferred_element_type=F32).astype(F16)
        part = lax.all_to_all(part.reshape(nz, nx * n, cols), "rows", split_axis=0, concat_axis=0, tiled=True)
        return jnp.sum(part.astype(F32), axis=0)

    first, second = reduced(mine), reduced(other)
    both = jnp.where(core == 0, jnp.stack([first, second]), jnp.stack([second, first]))
    both = both.astype(F16).reshape(nx, 2 * n, cols)
    logits = lax.all_to_all(both, "x", split_axis=0, concat_axis=0, tiled=True)
    logits = jnp.swapaxes(logits, 0, 1).reshape(2 * n, nx * cols).astype(F32)

    width = logits.shape[1]
    column = lax.axis_index(("y", "core")) * width + lax.broadcasted_iota(jnp.int32, logits.shape, 1)
    peak = jnp.max(logits, axis=1)
    total = jnp.sum(jnp.exp(logits - peak[:, None]), axis=1)
    picked = jnp.sum(jnp.where(column == tokens[:, None], logits, 0.0), axis=1)
    stats = spread(jnp.concatenate([peak, total, picked]), ("y", "core"), 2 * ny)
    peaks, totals, picks = jnp.split(stats, 3, axis=1)
    row_peak = jnp.max(peaks, axis=0)
    row_total = jnp.sum(totals * jnp.exp(peaks - row_peak), axis=0)
    shift = jnp.log(row_total)
    logprobs = logits - row_peak[:, None] - shift[:, None]
    target_logp = jnp.sum(picks, axis=0) - row_peak - shift
    return (logprobs, target_logp)


def solution(mesh):
    nv, nz, nx = mesh.devices.shape
    ny = nv // 2
    split = Mesh(mesh.devices.reshape(ny, 2, nz, nx), ("y", "core", "rows", "x"))
    in_specs = (P(("y", "core", "x"), "rows"), P("rows", ("y", "core", "x")), P(("rows", "x")))
    out_specs = (P(("rows", "x"), ("y", "core")), P(("rows", "x")))

    def body(*args):
        return local(ny, nz, nx, *args)

    return jax.shard_map(body, mesh=split, in_specs=in_specs, out_specs=out_specs, check_vma=False)
```

```python
import jax
import jax.numpy as jnp
from jax import lax
from jax.sharding import Mesh, PartitionSpec as P

F16 = jnp.float16
F32 = jnp.float32


def spread(x, axis, size):
    return lax.all_to_all(jnp.broadcast_to(x[None], (size,) + x.shape), axis, split_axis=0, concat_axis=0, tiled=True)


def local(ny, nz, nx, hidden, head_weight, tokens):
    n, k = hidden.shape
    m = n // 2
    cols = head_weight.shape[1]

    def reduced(rows):
        part = jnp.dot(rows, head_weight, preferred_element_type=F32).astype(F16)
        part = lax.all_to_all(part.reshape(nz * nx, 2 * m, cols), ("rows", "x"), split_axis=0, concat_axis=0, tiled=True)
        part = jnp.sum(part.reshape(nz, nx, 2 * m, cols).astype(F32), axis=0)
        return jnp.swapaxes(part, 0, 1).reshape(2, m, nx * cols)

    late = lax.all_gather(hidden[m:], ("y", "core", "x"), axis=0, tiled=True)
    early = spread(spread(spread(hidden[:m], "y", ny), "x", nx), "core", 2)
    early = jnp.transpose(early, (2, 0, 1, 3, 4)).reshape(ny * 2 * nx * m, k)
    logits = jnp.stack([reduced(early), reduced(late)], axis=1)

    width = nx * cols
    column = lax.axis_index(("y", "core")) * width + lax.broadcasted_iota(jnp.int32, logits.shape, 3)
    token = tokens.reshape(2, 2, m)
    peak = jnp.max(logits, axis=3)
    total = jnp.sum(jnp.exp(logits - peak[..., None]), axis=3)
    picked = jnp.sum(jnp.where(column == token[..., None], logits, 0.0), axis=3)
    stats = jnp.concatenate([peak.reshape(-1), total.reshape(-1), picked.reshape(-1)])
    peaks, totals, picks = jnp.split(spread(stats, ("y", "core"), 2 * ny), 3, axis=1)
    row_peak = jnp.max(peaks, axis=0)
    row_total = jnp.sum(totals * jnp.exp(peaks - row_peak), axis=0)
    shift = jnp.log(row_total)
    logprobs = logits.reshape(2 * n, width) - row_peak[:, None] - shift[:, None]
    target_logp = jnp.sum(picks, axis=0) - row_peak - shift
    return (logprobs, target_logp)


def solution(mesh):
    nv, nz, nx = mesh.devices.shape
    ny = nv // 2
    split = Mesh(mesh.devices.reshape(ny, 2, nz, nx), ("y", "core", "rows", "x"))
    in_specs = (P(("y", "core", "x"), "rows"), P("rows", ("y", "core", "x")), P(("rows", "x")))
    out_specs = (P(("rows", "x"), ("y", "core")), P(("rows", "x")))

    def body(*args):
        return local(ny, nz, nx, *args)

    return jax.shard_map(body, mesh=split, in_specs=in_specs, out_specs=out_specs, check_vma=False)
```

```python
import jax
import jax.numpy as jnp
from jax import lax
from jax.sharding import Mesh, PartitionSpec as P

F16 = jnp.float16
F32 = jnp.float32


def spread(x, axis, size):
    return lax.all_to_all(jnp.broadcast_to(x[None], (size,) + x.shape), axis, split_axis=0, concat_axis=0, tiled=True)


def local(ny, nz, nx, hidden, head_weight, tokens):
    n, k = hidden.shape
    cols = head_weight.shape[1]
    core, at = lax.axis_index("core"), lax.axis_index("x")

    base = spread(hidden, "y", ny)

    def product(mine):
        other = lax.ppermute(mine, "core", [(0, 1), (1, 0)])
        both = jnp.concatenate([mine, other], axis=1).reshape(ny * 2 * n, k)
        part = jnp.dot(both, head_weight, preferred_element_type=F32).astype(F16)
        return part.reshape(nz, 2 * n, cols)

    def summed(part):
        part = lax.all_to_all(part, "rows", split_axis=0, concat_axis=0, tiled=True)
        return jnp.sum(part.astype(F32), axis=0).reshape(2, 1, n, cols)

    sums = {}
    part = product(base)
    order = [0, 1, 3, 2]
    blocks = {s: lax.ppermute(base, "x", [(i, (i + s) % nx) for i in range(nx)]) for s in order[1:]}
    for s, after in zip(order, order[1:] + [None]):
        sums[s] = summed(part)
        if after is not None:
            mine, part = lax.optimization_barrier((blocks[after], part))
            part = product(mine)
    shape = (2, nx, n, cols)
    to_core = lax.broadcasted_iota(jnp.int32, shape, 0)
    to_x = lax.broadcasted_iota(jnp.int32, shape, 1)
    turned = jnp.zeros(shape, F32)
    for s in order:
        for o in range(2):
            here = (to_core == core ^ o) & (to_x == lax.rem(at + nx - s, nx))
            turned = jnp.where(here, sums[s][o], turned)
    turned = turned.astype(F16)
    logits = lax.all_to_all(turned.reshape(nx, 2 * n, cols), "x", split_axis=0, concat_axis=0, tiled=True)
    logits = jnp.swapaxes(logits, 0, 1).reshape(2 * n, nx * cols).astype(F32)

    width = logits.shape[1]
    column = lax.axis_index(("y", "core")) * width + lax.broadcasted_iota(jnp.int32, logits.shape, 1)
    peak = jnp.max(logits, axis=1)
    total = jnp.sum(jnp.exp(logits - peak[:, None]), axis=1)
    picked = jnp.sum(jnp.where(column == tokens[:, None], logits, 0.0), axis=1)
    stats = spread(jnp.concatenate([peak, total, picked]), ("y", "core"), 2 * ny)
    peaks, totals, picks = jnp.split(stats, 3, axis=1)
    row_peak = jnp.max(peaks, axis=0)
    row_total = jnp.sum(totals * jnp.exp(peaks - row_peak), axis=0)
    shift = jnp.log(row_total)
    logprobs = logits - row_peak[:, None] - shift[:, None]
    target_logp = jnp.sum(picks, axis=0) - row_peak - shift
    return (logprobs, target_logp)


def solution(mesh):
    nv, nz, nx = mesh.devices.shape
    ny = nv // 2
    split = Mesh(mesh.devices.reshape(ny, 2, nz, nx), ("y", "core", "rows", "x"))
    in_specs = (P(("y", "core", "x"), "rows"), P("rows", ("y", "core", "x")), P(("rows", "x")))
    out_specs = (P(("rows", "x"), ("y", "core")), P(("rows", "x")))

    def body(*args):
        return local(ny, nz, nx, *args)

    return jax.shard_map(body, mesh=split, in_specs=in_specs, out_specs=out_specs, check_vma=False)
```

```python
import jax
import jax.numpy as jnp
from jax import lax
from jax.sharding import Mesh, PartitionSpec as P

F16 = jnp.float16
F32 = jnp.float32
Y = ("yh", "yl")
Z = ("zh", "zl")


def spread(x, axis, size):
    return lax.all_to_all(jnp.broadcast_to(x[None], (size,) + x.shape), axis, split_axis=0, concat_axis=0, tiled=True)


def local(ny, nz, nx, hidden, head_weight, tokens):
    n, k = hidden.shape
    cols = head_weight.shape[1]
    half = cols // 2
    yh, zh = ny // 2, nz // 2
    core, odd = lax.axis_index("core"), lax.axis_index("zl")
    west = [(i, i ^ 1) for i in range(nz)]
    east = [(i, (i + 1) % nz if i % 2 else (i - 1) % nz) for i in range(nz)]

    mine = spread(spread(hidden, "yh", yh), ("yl", "x"), 2 * nx).reshape(2, nx, yh, n, k)
    give = lax.dynamic_index_in_dim(mine, 1 - odd, 0, keepdims=False)
    keep = lax.dynamic_index_in_dim(mine, odd, 0, keepdims=False)
    give_other = lax.ppermute(give, "core", [(0, 1), (1, 0)])
    keep_other = lax.ppermute(keep, "core", [(0, 1), (1, 0)])

    def product(own, other):
        place = lax.broadcasted_iota(jnp.int32, (2,) + own.shape, 0)
        rows = jnp.where(place == core, own[None], other[None])
        rows = jnp.transpose(rows, (2, 0, 1, 3, 4)).reshape(yh * 2 * nx * n, k)
        return jnp.dot(rows, head_weight, preferred_element_type=F32)

    given = product(give, give_other).astype(F16)
    left = lax.ppermute(given[:, :half], Z, west)
    right = lax.ppermute(given[:, half:], Z, east)
    kept = lax.optimization_barrier(product(keep, keep_other))
    pair = (kept + jnp.concatenate([left, right], axis=1).astype(F32)).astype(F16)
    part = lax.all_to_all(pair.reshape(zh * nx, 2 * n, cols), ("zh", "x"), split_axis=0, concat_axis=0, tiled=True)
    logits = jnp.sum(part.reshape(zh, nx, 2 * n, cols).astype(F32), axis=0)
    logits = jnp.swapaxes(logits, 0, 1).reshape(2 * n, nx * cols)

    width = logits.shape[1]
    column = lax.axis_index(Y + ("core",)) * width + lax.broadcasted_iota(jnp.int32, logits.shape, 1)
    peak = jnp.max(logits, axis=1)
    total = jnp.sum(jnp.exp(logits - peak[:, None]), axis=1)
    picked = jnp.sum(jnp.where(column == tokens[:, None], logits, 0.0), axis=1)
    stats, logits = lax.optimization_barrier((jnp.concatenate([peak, total, picked]), logits))
    peaks, totals, picks = jnp.split(spread(stats, Y + ("core",), 2 * ny), 3, axis=1)
    row_peak = jnp.max(peaks, axis=0)
    row_total = jnp.sum(totals * jnp.exp(peaks - row_peak), axis=0)
    shift = jnp.log(row_total)
    logprobs = logits - row_peak[:, None] - shift[:, None]
    target_logp = jnp.sum(picks, axis=0) - row_peak - shift
    return (logprobs, target_logp)


def solution(mesh):
    nv, nz, nx = mesh.devices.shape
    ny = nv // 2
    split = Mesh(mesh.devices.reshape(ny // 2, 2, 2, nz // 2, 2, nx), Y + ("core",) + Z + ("x",))
    in_specs = (P(Y + ("core", "x"), Z), P(Z, Y + ("core", "x")), P(Z + ("x",)))
    out_specs = (P(Z + ("x",), Y + ("core",)), P(Z + ("x",)))

    def body(*args):
        return local(ny, nz, nx, *args)

    return jax.shard_map(body, mesh=split, in_specs=in_specs, out_specs=out_specs, check_vma=False)
```

```python
import jax
import jax.numpy as jnp
from jax import lax
from jax.sharding import Mesh, PartitionSpec as P

F16 = jnp.float16
F32 = jnp.float32
Y = ("yh", "yl")
Z = ("zh", "zl")


def spread(x, axis, size):
    return lax.all_to_all(jnp.broadcast_to(x[None], (size,) + x.shape), axis, split_axis=0, concat_axis=0, tiled=True)


def local(ny, nz, nx, hidden, head_weight, tokens):
    n, k = hidden.shape
    cols = head_weight.shape[1]
    yh, zh = ny // 2, nz // 2
    core, odd, first = lax.axis_index("core"), lax.axis_index("zl"), lax.axis_index(Y + ("core",))
    hidden, tokens, core, odd, first = lax.optimization_barrier((hidden, tokens, core, odd, first * (nx * cols)))
    pairs = [(i, i ^ 1) for i in range(nz)]
    pairs += [(nz + i, nz + ((i + 1) % nz if i % 2 else (i - 1) % nz)) for i in range(nz)]

    mine = spread(spread(hidden, "yh", yh), ("yl", "x"), 2 * nx)
    other = lax.ppermute(mine, "core", [(0, 1), (1, 0)])

    def product(rows):
        part = jnp.dot(rows.reshape(2 * nx * yh * n, k), head_weight, preferred_element_type=F32)
        return part.astype(F16).reshape(2, nx, yh, n, cols)

    both = (product(mine), product(other))

    def parity(which):
        return jnp.stack([lax.dynamic_index_in_dim(p, which, 0, keepdims=False) for p in both])

    taken = lax.ppermute(parity(1 - odd), ("core",) + Z, pairs)
    pair = parity(odd).astype(F32) + taken.astype(F32)
    place = lax.broadcasted_iota(jnp.int32, pair.shape, 0)
    pair = jnp.where(place == core, pair[:1], pair[1:]).astype(F16)
    pair = jnp.transpose(pair, (2, 0, 1, 3, 4)).reshape(zh * nx, 2 * n, cols)
    part = lax.all_to_all(pair, ("zh", "x"), split_axis=0, concat_axis=0, tiled=True)
    logits = jnp.sum(part.reshape(zh, nx, 2 * n, cols).astype(F32), axis=0)
    logits = jnp.swapaxes(logits, 0, 1).reshape(2 * n, nx * cols)

    width = logits.shape[1]
    column = first + lax.broadcasted_iota(jnp.int32, logits.shape, 1)
    peak = jnp.max(logits, axis=1)
    total = jnp.sum(jnp.exp(logits - peak[:, None]), axis=1)
    picked = jnp.sum(jnp.where(column == tokens[:, None], logits, 0.0), axis=1)
    stats, logits = lax.optimization_barrier((jnp.concatenate([peak, total, picked]), logits))
    peaks, totals, picks = jnp.split(spread(stats, Y + ("core",), 2 * ny), 3, axis=1)
    row_peak = jnp.max(peaks, axis=0)
    row_total = jnp.sum(totals * jnp.exp(peaks - row_peak), axis=0)
    shift = jnp.log(row_total)
    logprobs = logits - row_peak[:, None] - shift[:, None]
    target_logp = jnp.sum(picks, axis=0) - row_peak - shift
    return (logprobs, target_logp)


def solution(mesh):
    nv, nz, nx = mesh.devices.shape
    ny = nv // 2
    split = Mesh(mesh.devices.reshape(ny // 2, 2, 2, nz // 2, 2, nx), Y + ("core",) + Z + ("x",))
    in_specs = (P(Y + ("core", "x"), Z), P(Z, Y + ("core", "x")), P(Z + ("x",)))
    out_specs = (P(Z + ("x",), Y + ("core",)), P(Z + ("x",)))

    def body(*args):
        return local(ny, nz, nx, *args)

    return jax.shard_map(body, mesh=split, in_specs=in_specs, out_specs=out_specs, check_vma=False)
```

```python
import jax
import jax.numpy as jnp
from jax import lax
from jax.sharding import Mesh, PartitionSpec as P

F16 = jnp.float16
F32 = jnp.float32
Y = ("yh", "yl")
Z = ("zh", "zl")


def spread(x, axis, size):
    return lax.all_to_all(jnp.broadcast_to(x[None], (size,) + x.shape), axis, split_axis=0, concat_axis=0, tiled=True)


def local(ny, nz, nx, hidden, head_weight, tokens):
    n, k = hidden.shape
    cols = head_weight.shape[1]
    yh, zh = ny // 2, nz // 2
    core, odd, block = lax.axis_index("core"), lax.axis_index("zl"), lax.axis_index(Y + ("core",))
    pairs = [(i, i ^ 1) for i in range(nz)]
    pairs += [(nz + i, nz + ((i + 1) % nz if i % 2 else (i - 1) % nz)) for i in range(nz)]
    token = tokens - block * (nx * cols)
    hidden, token, core, odd = lax.optimization_barrier((hidden, token, core, odd))

    mine = spread(spread(hidden, "yh", yh), ("yl", "x"), 2 * nx).reshape(2, nx, yh, n, k)
    mine = jnp.swapaxes(mine, 1, 2)
    other = lax.ppermute(mine, "core", [(0, 1), (1, 0)])

    def product(rows):
        part = jnp.dot(rows.reshape(2 * nx * yh * n, k), head_weight, preferred_element_type=F32)
        return part.astype(F16).reshape(2, yh, nx, n, cols)

    own, far = product(mine), product(other)

    def parity(which):
        a, b = (lax.dynamic_index_in_dim(p, which, 0, keepdims=True) for p in (own, far))
        place = lax.broadcasted_iota(jnp.int32, (2,) + a.shape[1:], 0)
        return jnp.where(place == core, a, b)

    taken = lax.ppermute(parity(1 - odd), ("core",) + Z, pairs)
    pair = (parity(odd).astype(F32) + taken.astype(F32)).astype(F16)
    pair = jnp.swapaxes(pair, 0, 1).reshape(zh * nx, 2 * n, cols)
    part = lax.all_to_all(pair, ("zh", "x"), split_axis=0, concat_axis=0, tiled=True)
    logits = jnp.sum(part.reshape(zh, nx, 2 * n, cols).astype(F32), axis=0)

    column = lax.broadcasted_iota(jnp.int32, logits.shape, 0) * cols + lax.broadcasted_iota(jnp.int32, logits.shape, 2)
    peak = jnp.max(logits, axis=(0, 2))
    total = jnp.sum(jnp.exp(logits - peak[:, None]), axis=(0, 2))
    picked = jnp.sum(jnp.where(column == token[:, None], logits, 0.0), axis=(0, 2))
    logits = jnp.swapaxes(logits, 0, 1).reshape(2 * n, nx * cols)
    stats, logits = lax.optimization_barrier((jnp.concatenate([peak, total, picked]), logits))
    peaks, totals, picks = jnp.split(spread(stats, Y + ("core",), 2 * ny), 3, axis=1)
    row_peak = jnp.max(peaks, axis=0)
    row_total = jnp.sum(totals * jnp.exp(peaks - row_peak), axis=0)
    shift = jnp.log(row_total)
    logprobs = logits - row_peak[:, None] - shift[:, None]
    target_logp = jnp.sum(picks, axis=0) - row_peak - shift
    return (logprobs, target_logp)


def solution(mesh):
    nv, nz, nx = mesh.devices.shape
    ny = nv // 2
    split = Mesh(mesh.devices.reshape(ny // 2, 2, 2, nz // 2, 2, nx), Y + ("core",) + Z + ("x",))
    in_specs = (P(Y + ("core", "x"), Z), P(Z, Y + ("core", "x")), P(Z + ("x",)))
    out_specs = (P(Z + ("x",), Y + ("core",)), P(Z + ("x",)))

    def body(*args):
        return local(ny, nz, nx, *args)

    return jax.shard_map(body, mesh=split, in_specs=in_specs, out_specs=out_specs, check_vma=False)
```

```python
import jax
import jax.numpy as jnp
from jax import lax
from jax.sharding import Mesh, PartitionSpec as P

F16 = jnp.float16
F32 = jnp.float32
Y = ("yh", "yl")
Z = ("zh", "zl")


def spread(x, axis, size):
    return lax.all_to_all(jnp.broadcast_to(x[None], (size,) + x.shape), axis, split_axis=0, concat_axis=0, tiled=True)


def local(ny, nz, nx, hidden, head_weight, tokens):
    n, k = hidden.shape
    cols = head_weight.shape[1]
    yh, zh = ny // 2, nz // 2
    core, odd, block = lax.axis_index("core"), lax.axis_index("zl"), lax.axis_index(Y + ("core",))
    pairs = [(i, i ^ 1) for i in range(nz)]
    pairs += [(nz + i, nz + ((i + 1) % nz if i % 2 else (i - 1) % nz)) for i in range(nz)]
    token = tokens - block * (nx * cols)
    hidden, token, core, odd = lax.optimization_barrier((hidden, token, core, odd))
    m, xh = n // 2, nx // 2

    def parity(own, far, which):
        a, b = (lax.dynamic_index_in_dim(p, which, 0, keepdims=True) for p in (own, far))
        place = lax.broadcasted_iota(jnp.int32, (2,) + a.shape[1:], 0)
        return jnp.where(place == core, a, b)

    def product(rows):
        part = jnp.dot(rows, head_weight, preferred_element_type=F32)
        return part.astype(F16).reshape(2, xh * yh, 2 * m, cols)

    def given(mine):
        mine = mine.reshape(xh, 2, 2, yh, m, k)
        mine = jnp.transpose(mine, (2, 0, 3, 1, 4, 5)).reshape(2 * nx * yh * m, k)
        mine = lax.optimization_barrier(mine)
        other = lax.ppermute(mine, "core", [(0, 1), (1, 0)])
        own, far = product(mine), product(other)
        return own, far, parity(own, far, 1 - odd)

    def paired(own, far, taken):
        return (parity(own, far, odd).astype(F32) + taken.astype(F32)).astype(F16)

    def summed(pair):
        part = lax.all_to_all(pair.reshape(nx * zh, 2 * m, cols), ("x", "zh"), split_axis=0, concat_axis=0, tiled=True)
        return jnp.sum(part.reshape(nx, zh, 2 * m, cols).astype(F32), axis=1)

    def local_stats(logits, token):
        column = lax.broadcasted_iota(jnp.int32, logits.shape, 0) * cols + lax.broadcasted_iota(jnp.int32, logits.shape, 2)
        peak = jnp.max(logits, axis=(0, 2))
        total = jnp.sum(jnp.exp(logits - peak[:, None]), axis=(0, 2))
        picked = jnp.sum(jnp.where(column == token[:, None], logits, 0.0), axis=(0, 2))
        return peak, total, picked

    near = spread(hidden, "yh", yh)
    gathered = [spread(near[:, h * m:(h + 1) * m], ("x", "yl"), 2 * nx) for h in range(2)]
    own, far, give = given(gathered[0])
    taken = lax.ppermute(give, ("core",) + Z, pairs)
    _, rows = lax.optimization_barrier((taken, gathered[1]))
    early = paired(own, far, taken)
    own, far, give = given(rows)
    give, _ = lax.optimization_barrier((give, early))
    taken = lax.ppermute(give, ("core",) + Z, pairs)
    logits = [summed(early), summed(paired(own, far, taken))]
    halves = [local_stats(v, token.reshape(2, 2, m)[:, h].reshape(2 * m)) for h, v in enumerate(logits)]
    stats = jnp.concatenate([jnp.concatenate(s) for s in zip(*halves)])
    stats, logits = lax.optimization_barrier((stats, logits))
    peaks, totals, picks = jnp.split(spread(stats, Y + ("core",), 2 * ny), 3, axis=1)
    row_peak = jnp.max(peaks, axis=0)
    row_total = jnp.sum(totals * jnp.exp(peaks - row_peak), axis=0)
    shift = jnp.log(row_total)
    target_logp = jnp.sum(picks, axis=0) - row_peak - shift
    target_logp = jnp.swapaxes(target_logp.reshape(2, 2, m), 0, 1).reshape(2 * n)
    outs = []
    for h, v in enumerate(logits):
        rows = slice(h * 2 * m, (h + 1) * 2 * m)
        v = v - row_peak[rows][:, None] - shift[rows][:, None]
        outs.append(jnp.swapaxes(v, 0, 1).reshape(2, m, nx * cols))
    logprobs = jnp.stack(outs, axis=1).reshape(2 * n, nx * cols)
    return (logprobs, target_logp)


def solution(mesh):
    nv, nz, nx = mesh.devices.shape
    ny = nv // 2
    split = Mesh(mesh.devices.reshape(ny // 2, 2, 2, nz // 2, 2, nx), Y + ("core",) + Z + ("x",))
    in_specs = (P(Y + ("core", "x"), Z), P(Z, Y + ("core", "x")), P(Z + ("x",)))
    out_specs = (P(Z + ("x",), Y + ("core",)), P(Z + ("x",)))

    def body(*args):
        return local(ny, nz, nx, *args)

    return jax.shard_map(body, mesh=split, in_specs=in_specs, out_specs=out_specs, check_vma=False)
```

```python
import jax
import jax.numpy as jnp
from jax import lax
from jax.sharding import Mesh, PartitionSpec as P

F16 = jnp.float16
F32 = jnp.float32
Y = ("yh", "yl")
Z = ("zh", "zl")


def spread(x, axis, size):
    return lax.all_to_all(jnp.broadcast_to(x[None], (size,) + x.shape), axis, split_axis=0, concat_axis=0, tiled=True)


def local(ny, nz, nx, hidden, head_weight, tokens):
    n, k = hidden.shape
    cols = head_weight.shape[1]
    yh, zh, xh = ny // 2, nz // 2, nx // 2
    core, odd, block = lax.axis_index("core"), lax.axis_index("zl"), lax.axis_index(Y + ("core",))
    pairs = [(i, i ^ 1) for i in range(nz)]
    pairs += [(nz + i, nz + ((i + 1) % nz if i % 2 else (i - 1) % nz)) for i in range(nz)]
    token = tokens - block * (nx * cols)
    hidden, token, core, odd = lax.optimization_barrier((hidden, token, core, odd))

    mine = spread(spread(hidden, "yh", yh), ("x", "yl"), 2 * nx).reshape(xh, 2, 2, yh, n, k)
    mine = jnp.transpose(mine, (2, 0, 3, 1, 4, 5)).reshape(2 * nx * yh * n, k)
    other = lax.ppermute(mine, "core", [(0, 1), (1, 0)])

    def product(rows):
        part = jnp.dot(rows, head_weight, preferred_element_type=F32)
        return part.astype(F16).reshape(2, xh * zh, 2 * n, cols)

    own, far = product(mine), product(other)

    def parity(which):
        a, b = (lax.dynamic_index_in_dim(p, which, 0, keepdims=True) for p in (own, far))
        place = lax.broadcasted_iota(jnp.int32, (2,) + a.shape[1:], 0)
        return jnp.where(place == core, a, b)

    taken = lax.ppermute(parity(1 - odd), ("core",) + Z, pairs)
    pair = (parity(odd).astype(F32) + taken.astype(F32)).astype(F16)
    part = lax.all_to_all(pair.reshape(nx * zh, 2 * n, cols), ("x", "zh"), split_axis=0, concat_axis=0, tiled=True)
    logits = jnp.sum(part.reshape(nx, zh, 2 * n, cols).astype(F32), axis=1)

    column = lax.broadcasted_iota(jnp.int32, logits.shape, 0) * cols + lax.broadcasted_iota(jnp.int32, logits.shape, 2)
    peak = jnp.max(logits, axis=(0, 2))
    total = jnp.sum(jnp.exp(logits - peak[:, None]), axis=(0, 2))
    picked = jnp.sum(jnp.where(column == token[:, None], logits, 0.0), axis=(0, 2))
    logits = jnp.swapaxes(logits, 0, 1).reshape(2 * n, nx * cols)
    stats, logits = lax.optimization_barrier((jnp.concatenate([peak, total, picked]), logits))
    peaks, totals, picks = jnp.split(spread(stats, ("core", "yl", "yh"), 2 * ny), 3, axis=1)
    row_peak = jnp.max(peaks, axis=0)
    row_total = jnp.sum(totals * jnp.exp(peaks - row_peak), axis=0)
    shift = jnp.log(row_total)
    logprobs = logits - row_peak[:, None] - shift[:, None]
    target_logp = jnp.sum(picks, axis=0) - row_peak - shift
    return (logprobs, target_logp)


def solution(mesh):
    nv, nz, nx = mesh.devices.shape
    ny = nv // 2
    split = Mesh(mesh.devices.reshape(ny // 2, 2, 2, nz // 2, 2, nx), Y + ("core",) + Z + ("x",))
    in_specs = (P(Y + ("core", "x"), Z), P(Z, Y + ("core", "x")), P(Z + ("x",)))
    out_specs = (P(Z + ("x",), Y + ("core",)), P(Z + ("x",)))

    def body(*args):
        return local(ny, nz, nx, *args)

    return jax.shard_map(body, mesh=split, in_specs=in_specs, out_specs=out_specs, check_vma=False)
```

```python
import jax
import jax.numpy as jnp
from jax import lax
from jax.sharding import Mesh, PartitionSpec as P

F16 = jnp.float16
F32 = jnp.float32
Y = ("yh", "yl")
Z = ("zh", "zl")


def spread(x, axis, size):
    return lax.all_to_all(jnp.broadcast_to(x[None], (size,) + x.shape), axis, split_axis=0, concat_axis=0, tiled=True)


def local(ny, nz, nx, hidden, head_weight, tokens):
    n, k = hidden.shape
    cols = head_weight.shape[1]
    yh, zh, xh = ny // 2, nz // 2, nx // 2
    core, odd, block = lax.axis_index("core"), lax.axis_index("zl"), lax.axis_index(Y + ("core",))
    pairs = [(i, i ^ 1) for i in range(nz)]
    pairs += [(nz + i, nz + ((i + 1) % nz if i % 2 else (i - 1) % nz)) for i in range(nz)]
    hidden, core, odd, block = lax.optimization_barrier((hidden, core, odd, block))

    mine = spread(spread(hidden, "yh", yh), ("x", "yl"), 2 * nx).reshape(xh, 2, 2, yh, n, k)
    mine = jnp.transpose(mine, (2, 0, 3, 1, 4, 5)).reshape(2 * nx * yh * n, k)
    mine, tokens = lax.optimization_barrier((mine, tokens))
    other = lax.ppermute(mine, "core", [(0, 1), (1, 0)])
    token_block = tokens // cols - block * nx
    token_column = lax.rem(tokens, cols)

    def product(rows):
        part = jnp.dot(rows, head_weight, preferred_element_type=F32)
        return part.astype(F16).reshape(2, xh * zh, 2 * n, cols)

    own, far = product(mine), product(other)

    def parity(which):
        a, b = (lax.dynamic_index_in_dim(p, which, 0, keepdims=True) for p in (own, far))
        place = lax.broadcasted_iota(jnp.int32, (2,) + a.shape[1:], 0)
        return jnp.where(place == core, a, b)

    taken = lax.ppermute(parity(1 - odd), ("core",) + Z, pairs)
    pair = (parity(odd).astype(F32) + taken.astype(F32)).astype(F16)
    pair, token_block, token_column = lax.optimization_barrier((pair, token_block, token_column))
    part = lax.all_to_all(pair.reshape(nx * zh, 2 * n, cols), ("x", "zh"), split_axis=0, concat_axis=0, tiled=True)
    logits = jnp.sum(part.reshape(nx, zh, 2 * n, cols).astype(F32), axis=1)

    hit = lax.broadcasted_iota(jnp.int32, logits.shape, 0) == token_block[:, None]
    hit &= lax.broadcasted_iota(jnp.int32, logits.shape, 2) == token_column[:, None]
    peak = jnp.max(logits, axis=(0, 2))
    total = jnp.sum(jnp.exp(logits - peak[:, None]), axis=(0, 2))
    picked = jnp.sum(jnp.where(hit, logits, 0.0), axis=(0, 2))
    logits = jnp.swapaxes(logits, 0, 1).reshape(2 * n, nx * cols)
    stats, logits = lax.optimization_barrier((jnp.concatenate([peak, total, picked]), logits))
    peaks, totals, picks = jnp.split(spread(stats, ("core", "yl", "yh"), 2 * ny), 3, axis=1)
    row_peak = jnp.max(peaks, axis=0)
    row_total = jnp.sum(totals * jnp.exp(peaks - row_peak), axis=0)
    shift = jnp.log(row_total)
    logprobs = logits - row_peak[:, None] - shift[:, None]
    target_logp = jnp.sum(picks, axis=0) - row_peak - shift
    return (logprobs, target_logp)


def solution(mesh):
    nv, nz, nx = mesh.devices.shape
    ny = nv // 2
    split = Mesh(mesh.devices.reshape(ny // 2, 2, 2, nz // 2, 2, nx), Y + ("core",) + Z + ("x",))
    in_specs = (P(Y + ("core", "x"), Z), P(Z, Y + ("core", "x")), P(Z + ("x",)))
    out_specs = (P(Z + ("x",), Y + ("core",)), P(Z + ("x",)))

    def body(*args):
        return local(ny, nz, nx, *args)

    return jax.shard_map(body, mesh=split, in_specs=in_specs, out_specs=out_specs, check_vma=False)
```

```python
import jax
import jax.numpy as jnp
from jax import lax
from jax.sharding import Mesh, PartitionSpec as P

F16 = jnp.float16
F32 = jnp.float32
Y = ("yh", "yl")
Z = ("zh", "zl")


def spread(x, axis, size):
    return lax.all_to_all(jnp.broadcast_to(x[None], (size,) + x.shape), axis, split_axis=0, concat_axis=0, tiled=True)


def local(ny, nz, nx, hidden, head_weight, tokens):
    n, k = hidden.shape
    cols = head_weight.shape[1]
    yh, zh, xh = ny // 2, nz // 2, nx // 2
    core, odd, block = lax.axis_index("core"), lax.axis_index("zl"), lax.axis_index(Y + ("core",))
    pairs = [(i, i ^ 1) for i in range(nz)]
    pairs += [(nz + i, nz + ((i + 1) % nz if i % 2 else (i - 1) % nz)) for i in range(nz)]
    hidden, core, odd, block = lax.optimization_barrier((hidden, core, odd, block))

    mine = spread(spread(hidden, "yh", yh), ("x", "yl"), 2 * nx).reshape(xh, 2, 2, yh, n, k)
    mine = jnp.transpose(mine, (2, 0, 3, 1, 4, 5)).reshape(2 * nx * yh * n, k)
    mine, tokens = lax.optimization_barrier((mine, tokens))
    other = lax.ppermute(mine, "core", [(0, 1), (1, 0)])
    token_block = tokens // cols - block * nx
    token_column = lax.rem(tokens, cols)

    def product(rows):
        part = jnp.dot(rows, head_weight, preferred_element_type=F32)
        return part.astype(F16).reshape(2, xh * zh, 2 * n, cols)

    def parity(part, which):
        return lax.dynamic_index_in_dim(part, which, 0, keepdims=False)

    def partner(part):
        return lax.ppermute(part, ("core",) + Z, pairs)

    own = product(mine)
    give = parity(own, 1 - odd)
    other, _ = lax.optimization_barrier((other, give))
    far = product(other)
    own = parity(own, odd).astype(F32) + partner(give).astype(F32)
    far = parity(far, odd).astype(F32) + partner(parity(far, 1 - odd)).astype(F32)
    place = lax.broadcasted_iota(jnp.int32, (2,) + own.shape, 0)
    pair = jnp.where(place == core, own[None], far[None]).astype(F16)
    pair, token_block, token_column = lax.optimization_barrier((pair, token_block, token_column))
    part = lax.all_to_all(pair.reshape(nx * zh, 2 * n, cols), ("x", "zh"), split_axis=0, concat_axis=0, tiled=True)
    logits = jnp.sum(part.reshape(nx, zh, 2 * n, cols).astype(F32), axis=1)

    hit = lax.broadcasted_iota(jnp.int32, logits.shape, 0) == token_block[:, None]
    hit &= lax.broadcasted_iota(jnp.int32, logits.shape, 2) == token_column[:, None]
    peak = jnp.max(logits, axis=(0, 2))
    total = jnp.sum(jnp.exp(logits - peak[:, None]), axis=(0, 2))
    picked = jnp.sum(jnp.where(hit, logits, 0.0), axis=(0, 2))
    logits = jnp.swapaxes(logits, 0, 1).reshape(2 * n, nx * cols)
    stats, logits = lax.optimization_barrier((jnp.concatenate([peak, total, picked]), logits))
    peaks, totals, picks = jnp.split(spread(stats, ("core", "yl", "yh"), 2 * ny), 3, axis=1)
    row_peak = jnp.max(peaks, axis=0)
    row_total = jnp.sum(totals * jnp.exp(peaks - row_peak), axis=0)
    shift = jnp.log(row_total)
    logprobs = logits - row_peak[:, None] - shift[:, None]
    target_logp = jnp.sum(picks, axis=0) - row_peak - shift
    return (logprobs, target_logp)


def solution(mesh):
    nv, nz, nx = mesh.devices.shape
    ny = nv // 2
    split = Mesh(mesh.devices.reshape(ny // 2, 2, 2, nz // 2, 2, nx), Y + ("core",) + Z + ("x",))
    in_specs = (P(Y + ("core", "x"), Z), P(Z, Y + ("core", "x")), P(Z + ("x",)))
    out_specs = (P(Z + ("x",), Y + ("core",)), P(Z + ("x",)))

    def body(*args):
        return local(ny, nz, nx, *args)

    return jax.shard_map(body, mesh=split, in_specs=in_specs, out_specs=out_specs, check_vma=False)
```

```python
import jax
import jax.numpy as jnp
from jax import lax
from jax.sharding import Mesh, PartitionSpec as P

F16 = jnp.float16
F32 = jnp.float32
Y = ("yh", "yl")
Z = ("zh", "zl")


def spread(x, axis, size):
    return lax.all_to_all(jnp.broadcast_to(x[None], (size,) + x.shape), axis, split_axis=0, concat_axis=0, tiled=True)


def local(ny, nz, nx, hidden, head_weight, tokens):
    n, k = hidden.shape
    cols = head_weight.shape[1]
    yh, zh, xh = ny // 2, nz // 2, nx // 2
    core, odd, block = lax.axis_index("core"), lax.axis_index("zl"), lax.axis_index(Y + ("core",))
    pairs = [(i, i ^ 1) for i in range(nz)]
    pairs += [(nz + i, nz + ((i + 1) % nz if i % 2 else (i - 1) % nz)) for i in range(nz)]
    hidden, core, odd, block = lax.optimization_barrier((hidden, core, odd, block * nx))

    mine = spread(spread(hidden, "yh", yh), ("x", "yl"), 2 * nx).reshape(xh, 2, 2, yh, n, k)
    mine, tokens, core, odd, block = lax.optimization_barrier((mine, tokens, core, odd, block))
    token_block = tokens // cols - block
    token_column = lax.rem(tokens, cols)

    def parity(which):
        rows = lax.dynamic_index_in_dim(mine, which, 2, keepdims=False)
        return jnp.swapaxes(rows, 1, 2).reshape(nx * yh * n, k)

    def product(rows):
        part = jnp.dot(rows, head_weight, preferred_element_type=F32)
        return part.reshape(xh * zh, 2 * n, cols)

    def swapped(rows):
        return lax.ppermute(rows, "core", [(0, 1), (1, 0)])

    def partner(part):
        return lax.ppermute(part.astype(F16), ("core",) + Z, pairs).astype(F32)

    give, keep = lax.optimization_barrier((parity(1 - odd), parity(odd)))
    give_far = swapped(give)
    given = product(give).astype(F16)
    give_far, _ = lax.optimization_barrier((give_far, given))
    given_far = product(give_far).astype(F16)
    taken, taken_far = partner(given), partner(given_far)
    keep, _ = lax.optimization_barrier((keep, taken))
    kept, kept_far = lax.optimization_barrier((product(keep), product(swapped(keep))))
    own, far = kept + taken, kept_far + taken_far
    place = lax.broadcasted_iota(jnp.int32, (2,) + own.shape, 0)
    pair = jnp.where(place == core, own[None], far[None]).astype(F16)
    pair, token_block, token_column = lax.optimization_barrier((pair, token_block, token_column))
    part = lax.all_to_all(pair.reshape(nx * zh, 2 * n, cols), ("x", "zh"), split_axis=0, concat_axis=0, tiled=True)
    logits = jnp.sum(part.reshape(nx, zh, 2 * n, cols).astype(F32), axis=1)

    hit = lax.broadcasted_iota(jnp.int32, logits.shape, 0) == token_block[:, None]
    hit &= lax.broadcasted_iota(jnp.int32, logits.shape, 2) == token_column[:, None]
    peak = jnp.max(logits, axis=(0, 2))
    total = jnp.sum(jnp.exp(logits - peak[:, None]), axis=(0, 2))
    picked = jnp.sum(jnp.where(hit, logits, 0.0), axis=(0, 2))
    logits = jnp.swapaxes(logits, 0, 1).reshape(2 * n, nx * cols)
    stats, logits = lax.optimization_barrier((jnp.concatenate([peak, total, picked]), logits))
    peaks, totals, picks = jnp.split(spread(stats, ("core", "yl", "yh"), 2 * ny), 3, axis=1)
    row_peak = jnp.max(peaks, axis=0)
    row_total = jnp.sum(totals * jnp.exp(peaks - row_peak), axis=0)
    shift = jnp.log(row_total)
    logprobs = logits - row_peak[:, None] - shift[:, None]
    target_logp = jnp.sum(picks, axis=0) - row_peak - shift
    return (logprobs, target_logp)


def solution(mesh):
    nv, nz, nx = mesh.devices.shape
    ny = nv // 2
    split = Mesh(mesh.devices.reshape(ny // 2, 2, 2, nz // 2, 2, nx), Y + ("core",) + Z + ("x",))
    in_specs = (P(Y + ("core", "x"), Z), P(Z, Y + ("core", "x")), P(Z + ("x",)))
    out_specs = (P(Z + ("x",), Y + ("core",)), P(Z + ("x",)))

    def body(*args):
        return local(ny, nz, nx, *args)

    return jax.shard_map(body, mesh=split, in_specs=in_specs, out_specs=out_specs, check_vma=False)
```

```python
import jax
import jax.numpy as jnp
from jax import lax
from jax.sharding import Mesh, PartitionSpec as P

F16 = jnp.float16
F32 = jnp.float32
Y = ("yh", "yl")
Z = ("zh", "zl")


def spread(x, axis, size):
    return lax.all_to_all(jnp.broadcast_to(x[None], (size,) + x.shape), axis, split_axis=0, concat_axis=0, tiled=True)


def local(ny, nz, nx, hidden, head_weight, tokens):
    n, k = hidden.shape
    cols = head_weight.shape[1]
    yh, zh, xh = ny // 2, nz // 2, nx // 2
    core, odd, block = lax.axis_index("core"), lax.axis_index("zl"), lax.axis_index(Y + ("core",))
    pairs = [(i, i ^ 1) for i in range(nz)]
    pairs += [(nz + i, nz + ((i + 1) % nz if i % 2 else (i - 1) % nz)) for i in range(nz)]
    hidden, core, odd, block = lax.optimization_barrier((hidden, core, odd, block * nx))

    mine = spread(spread(hidden, "yh", yh), ("x", "yl"), 2 * nx).reshape(xh, 2, 2, yh, n, k)
    mine, tokens, core, odd, block = lax.optimization_barrier((mine, tokens, core, odd, block))
    token_block = tokens // cols - block
    token_column = lax.rem(tokens, cols)

    def parity(which):
        rows = lax.dynamic_index_in_dim(mine, which, 2, keepdims=False)
        return jnp.swapaxes(rows, 1, 2).reshape(nx * yh * n, k)

    def product(rows):
        part = jnp.dot(rows, head_weight, preferred_element_type=F32)
        return part.reshape(xh * zh, 2 * n, cols)

    def swapped(rows):
        return lax.ppermute(rows, "core", [(0, 1), (1, 0)])

    def partner(part):
        return lax.ppermute(part, ("core",) + Z, pairs)

    give, keep = lax.optimization_barrier((parity(1 - odd), parity(odd)))
    give_far = swapped(give)
    given = product(give).astype(F16)
    taken = partner(given)
    keep, given = lax.optimization_barrier((keep, given))
    taken_far = partner(product(give_far).astype(F16))
    kept, kept_far = lax.optimization_barrier((product(keep), product(swapped(keep))))
    own, far = kept + taken.astype(F32), kept_far + taken_far.astype(F32)
    place = lax.broadcasted_iota(jnp.int32, (2,) + own.shape, 0)
    pair = jnp.where(place == core, own[None], far[None]).astype(F16)
    pair, token_block, token_column = lax.optimization_barrier((pair, token_block, token_column))
    part = lax.all_to_all(pair.reshape(nx * zh, 2 * n, cols), ("x", "zh"), split_axis=0, concat_axis=0, tiled=True)
    logits = jnp.sum(part.reshape(nx, zh, 2 * n, cols).astype(F32), axis=1)

    hit = lax.broadcasted_iota(jnp.int32, logits.shape, 0) == token_block[:, None]
    hit &= lax.broadcasted_iota(jnp.int32, logits.shape, 2) == token_column[:, None]
    peak = jnp.max(logits, axis=(0, 2))
    total = jnp.sum(jnp.exp(logits - peak[:, None]), axis=(0, 2))
    picked = jnp.sum(jnp.where(hit, logits, 0.0), axis=(0, 2))
    logits = jnp.swapaxes(logits, 0, 1).reshape(2 * n, nx * cols)
    stats, logits = lax.optimization_barrier((jnp.concatenate([peak, total, picked]), logits))
    peaks, totals, picks = jnp.split(spread(stats, ("core", "yl", "yh"), 2 * ny), 3, axis=1)
    row_peak = jnp.max(peaks, axis=0)
    row_total = jnp.sum(totals * jnp.exp(peaks - row_peak), axis=0)
    shift = jnp.log(row_total)
    logprobs = logits - row_peak[:, None] - shift[:, None]
    target_logp = jnp.sum(picks, axis=0) - row_peak - shift
    return (logprobs, target_logp)


def solution(mesh):
    nv, nz, nx = mesh.devices.shape
    ny = nv // 2
    split = Mesh(mesh.devices.reshape(ny // 2, 2, 2, nz // 2, 2, nx), Y + ("core",) + Z + ("x",))
    in_specs = (P(Y + ("core", "x"), Z), P(Z, Y + ("core", "x")), P(Z + ("x",)))
    out_specs = (P(Z + ("x",), Y + ("core",)), P(Z + ("x",)))

    def body(*args):
        return local(ny, nz, nx, *args)

    return jax.shard_map(body, mesh=split, in_specs=in_specs, out_specs=out_specs, check_vma=False)
```

```python
import jax
import jax.numpy as jnp
from jax import lax
from jax.sharding import Mesh, PartitionSpec as P

F16 = jnp.float16
F32 = jnp.float32
Y = ("yh", "yl")
Z = ("zh", "zl")


def spread(x, axis, size):
    return lax.all_to_all(jnp.broadcast_to(x[None], (size,) + x.shape), axis, split_axis=0, concat_axis=0, tiled=True)


def local(ny, nz, nx, hidden, head_weight, tokens):
    n, k = hidden.shape
    cols = head_weight.shape[1]
    yh, zh, xh = ny // 2, nz // 2, nx // 2
    core, odd, block = lax.axis_index("core"), lax.axis_index("zl"), lax.axis_index(Y + ("core",))
    pairs = [(i, i ^ 1) for i in range(nz)]
    pairs += [(nz + i, nz + ((i + 1) % nz if i % 2 else (i - 1) % nz)) for i in range(nz)]
    hidden, core, odd, block = lax.optimization_barrier((hidden, core, odd, block * nx))

    mine = spread(spread(hidden, "yh", yh), ("x", "yl"), 2 * nx).reshape(xh, 2, 2, yh, n, k)
    mine, tokens, core, odd, block = lax.optimization_barrier((mine, tokens, core, odd, block))
    token_block = tokens // cols - block
    token_column = lax.rem(tokens, cols)

    def parity(which):
        rows = lax.dynamic_index_in_dim(mine, which, 2, keepdims=False)
        return jnp.transpose(rows, (2, 0, 1, 3, 4)).reshape(nx * yh * n, k)

    def product(rows):
        part = jnp.dot(rows, head_weight, preferred_element_type=F32)
        return part.reshape(zh, xh, 2 * n, cols)

    def swapped(rows):
        return lax.ppermute(rows, "core", [(0, 1), (1, 0)])

    def partner(part):
        return lax.ppermute(part.astype(F16), ("core",) + Z, pairs).astype(F32)

    give, keep = lax.optimization_barrier((parity(1 - odd), parity(odd)))
    give_far = swapped(give)
    given = product(give).astype(F16)
    give_far, _ = lax.optimization_barrier((give_far, given))
    given_far = product(give_far).astype(F16)
    taken, taken_far = partner(given), partner(given_far)
    keep, _ = lax.optimization_barrier((keep, taken))
    kept, kept_far = lax.optimization_barrier((product(keep), product(swapped(keep))))
    own, far = kept + taken, kept_far + taken_far
    place = lax.broadcasted_iota(jnp.int32, (2,) + own.shape, 0)
    pair = jnp.swapaxes(jnp.where(place == core, own[None], far[None]).astype(F16), 0, 1)
    pair, token_block, token_column = lax.optimization_barrier((pair, token_block, token_column))
    part = lax.all_to_all(pair.reshape(zh * nx, 2 * n, cols), ("zh", "x"), split_axis=0, concat_axis=0, tiled=True)
    logits = jnp.sum(part.reshape(zh, nx, 2 * n, cols).astype(F32), axis=0)

    hit = lax.broadcasted_iota(jnp.int32, logits.shape, 0) == token_block[:, None]
    hit &= lax.broadcasted_iota(jnp.int32, logits.shape, 2) == token_column[:, None]
    peak = jnp.max(logits, axis=(0, 2))
    total = jnp.sum(jnp.exp(logits - peak[:, None]), axis=(0, 2))
    picked = jnp.sum(jnp.where(hit, logits, 0.0), axis=(0, 2))
    logits = jnp.swapaxes(logits, 0, 1).reshape(2 * n, nx * cols)
    stats, logits = lax.optimization_barrier((jnp.concatenate([peak, total, picked]), logits))
    peaks, totals, picks = jnp.split(spread(stats, ("core", "yl", "yh"), 2 * ny), 3, axis=1)
    row_peak = jnp.max(peaks, axis=0)
    row_total = jnp.sum(totals * jnp.exp(peaks - row_peak), axis=0)
    shift = jnp.log(row_total)
    logprobs = logits - row_peak[:, None] - shift[:, None]
    target_logp = jnp.sum(picks, axis=0) - row_peak - shift
    return (logprobs, target_logp)


def solution(mesh):
    nv, nz, nx = mesh.devices.shape
    ny = nv // 2
    split = Mesh(mesh.devices.reshape(ny // 2, 2, 2, nz // 2, 2, nx), Y + ("core",) + Z + ("x",))
    in_specs = (P(Y + ("core", "x"), Z), P(Z, Y + ("core", "x")), P(Z + ("x",)))
    out_specs = (P(Z + ("x",), Y + ("core",)), P(Z + ("x",)))

    def body(*args):
        return local(ny, nz, nx, *args)

    return jax.shard_map(body, mesh=split, in_specs=in_specs, out_specs=out_specs, check_vma=False)
```

```python
import jax
import jax.numpy as jnp
from jax import lax
from jax.sharding import Mesh, PartitionSpec as P

F16 = jnp.float16
F32 = jnp.float32
Y = ("yh", "yl")
Z = ("zh", "zl")


def spread(x, axis, size):
    return lax.all_to_all(jnp.broadcast_to(x[None], (size,) + x.shape), axis, split_axis=0, concat_axis=0, tiled=True)


def local(ny, nz, nx, hidden, head_weight, tokens):
    n, k = hidden.shape
    cols = head_weight.shape[1]
    yh, zh, xh = ny // 2, nz // 2, nx // 2
    core, odd, block = lax.axis_index("core"), lax.axis_index("zl"), lax.axis_index(Y + ("core",))
    pairs = [(i, i ^ 1) for i in range(nz)]
    pairs += [(nz + i, nz + ((i + 1) % nz if i % 2 else (i - 1) % nz)) for i in range(nz)]
    hidden, core, odd, block = lax.optimization_barrier((hidden, core, odd, block * nx))

    mine = spread(spread(hidden, ("yl", "yh"), ny), "x", nx).reshape(xh, 2, 2, yh, n, k)
    mine, tokens, core, odd, block = lax.optimization_barrier((mine, tokens, core, odd, block))
    token_block = tokens // cols - block
    token_column = lax.rem(tokens, cols)

    def parity(which):
        rows = lax.dynamic_index_in_dim(mine, which, 2, keepdims=False)
        return jnp.swapaxes(rows, 1, 2).reshape(nx * yh * n, k)

    def product(rows):
        part = jnp.dot(rows, head_weight, preferred_element_type=F32)
        return part.reshape(xh * zh, 2 * n, cols)

    def swapped(rows):
        return lax.ppermute(rows, "core", [(0, 1), (1, 0)])

    def partner(part):
        return lax.ppermute(part.astype(F16), ("core",) + Z, pairs).astype(F32)

    give, keep = lax.optimization_barrier((parity(1 - odd), parity(odd)))
    give_far = swapped(give)
    given = product(give).astype(F16)
    give_far, _ = lax.optimization_barrier((give_far, given))
    given_far = product(give_far).astype(F16)
    taken, taken_far = partner(given), partner(given_far)
    keep, _ = lax.optimization_barrier((keep, taken))
    kept, kept_far = lax.optimization_barrier((product(keep), product(swapped(keep))))
    own, far = kept + taken, kept_far + taken_far
    place = lax.broadcasted_iota(jnp.int32, (2,) + own.shape, 0)
    pair = jnp.where(place == core, own[None], far[None]).astype(F16)
    pair, token_block, token_column = lax.optimization_barrier((pair, token_block, token_column))
    part = lax.all_to_all(pair.reshape(nx * zh, 2 * n, cols), ("x", "zh"), split_axis=0, concat_axis=0, tiled=True)
    logits = jnp.sum(part.reshape(nx, zh, 2 * n, cols).astype(F32), axis=1)

    hit = lax.broadcasted_iota(jnp.int32, logits.shape, 0) == token_block[:, None]
    hit &= lax.broadcasted_iota(jnp.int32, logits.shape, 2) == token_column[:, None]
    peak = jnp.max(logits, axis=(0, 2))
    total = jnp.sum(jnp.exp(logits - peak[:, None]), axis=(0, 2))
    picked = jnp.sum(jnp.where(hit, logits, 0.0), axis=(0, 2))
    logits = jnp.swapaxes(logits, 0, 1).reshape(2 * n, nx * cols)
    stats, logits = lax.optimization_barrier((jnp.concatenate([peak, total, picked]), logits))
    peaks, totals, picks = jnp.split(spread(stats, ("core", "yl", "yh"), 2 * ny), 3, axis=1)
    row_peak = jnp.max(peaks, axis=0)
    row_total = jnp.sum(totals * jnp.exp(peaks - row_peak), axis=0)
    shift = jnp.log(row_total)
    logprobs = logits - row_peak[:, None] - shift[:, None]
    target_logp = jnp.sum(picks, axis=0) - row_peak - shift
    return (logprobs, target_logp)


def solution(mesh):
    nv, nz, nx = mesh.devices.shape
    ny = nv // 2
    split = Mesh(mesh.devices.reshape(ny // 2, 2, 2, nz // 2, 2, nx), Y + ("core",) + Z + ("x",))
    in_specs = (P(Y + ("core", "x"), Z), P(Z, Y + ("core", "x")), P(Z + ("x",)))
    out_specs = (P(Z + ("x",), Y + ("core",)), P(Z + ("x",)))

    def body(*args):
        return local(ny, nz, nx, *args)

    return jax.shard_map(body, mesh=split, in_specs=in_specs, out_specs=out_specs, check_vma=False)
```
